512 devices in a mesh: line: 8 (over y_hi, x), bus: 32 (over y_lo, z), scen: 2 (over core).
Axes of the slice: x: 4, y: 4 (y_hi: 2, y_lo: 2; y = y_hi * 2 + y_lo), z: 16, core: 2. Of those that a mesh axis runs over, the one named last changes fastest.
Arguments:
- ptdf: bfloat16 [8192, 49152], P('line', 'bus'), may hold values from -0.0546875 to 0.0546875
- injections: bfloat16 [49152, 512], P('bus', 'scen'), may hold values from -6 to 6
- lodf: bfloat16 [8192, 2048], P(('line', 'bus')), may hold values from -3 to 3
- ratings: float32 [8192], P(('line', 'bus')), may hold values from 0.5 to 2
- outages: int32 [2048], replicated, may hold values from 0 to 8191, as said below
Outputs:
- overload: float32 [8192, 2048], P(('line', 'bus'))
The draws below stay inside these ranges and needn't reach their ends.
Inputs may be any that keep to these rules, and one draw needn't show every extreme that they name: `outages`: 2048 distinct line indices.
All inputs are finite; a program needn't handle non-finite values.
Results may differ from the reference program's by a relative error of at most 0.0003.
Values sent between devices are 32-bit elements; how exact they have to be, the bound alone decides.
No kernel may reach another device: no remote copies, remote signals or barrier semaphores. Data moves between devices by JAX's collectives and lax.ppermute only.
A program may use at most 64 MiB of HBM per device.

```python
import math
import jax
import jax.numpy as jnp
from jax import lax

ROWS_DEV = 32
SCEN_DEV = 256
BUSES = 49152
LINES = 8192
OUTAGES = 2048
SCENARIOS = 512
N_LINE = 8
N_BUS = 32
N_SCEN = 2


def draw_outages(key, part):
    line_count = ROWS_DEV * N_LINE * N_BUS
    picked = line_count // 4
    middle = jax.random.permutation(jax.random.fold_in(key, 17), line_count - 2) + 1
    chosen = jnp.concatenate([middle[:picked - 2].astype(jnp.int32), jnp.array([0, line_count - 1], jnp.int32)])
    shuffled = jax.random.permutation(jax.random.fold_in(key, 29), chosen)
    return shuffled.astype(jnp.int32)


def with_spikes(drawn, key, source, target, shards_of, factor):
    owner, partner = [(jnp.arange(drawn.shape[position]) // (drawn.shape[position] // shards_of)).reshape([-1 if axis == position else 1 for axis in range(drawn.ndim)]) for position in (source, target)]
    chosen = jax.random.permutation(key, shards_of)[partner]
    strong = (owner == chosen) | (owner == (partner + shards_of // 2) % shards_of)
    return jnp.where(strong, factor * drawn, drawn)


def steps_of(rng, extent, shards, smallest, largest):
    level = 1.0
    for axis_at, shards_of in shards:
        draws = jax.random.uniform(jax.random.fold_in(jax.random.fold_in(rng, 6), axis_at), (shards_of,), jnp.float32, smallest / len(shards), largest / len(shards))
        level = level * jnp.repeat(jnp.exp(draws), extent[axis_at] // shards_of).reshape((-1,) + (1,) * (len(extent) - 1 - axis_at))
    return level


def centred(rng, extent, scale, most, cuts=(), kind=jnp.bfloat16):
    loudness = steps_of(rng, extent, cuts, -0.22, 0.18) if cuts else 1.0
    result = jax.random.normal(rng, extent, jnp.float32) * scale * loudness
    return jnp.minimum(jnp.maximum(result, -most), most).astype(kind)


def gaussian_with(own_key, dims, scale, most, cuts, heavy, kind=jnp.bfloat16):
    entries = scale * jax.random.normal(own_key, dims, jnp.float32)
    if cuts:
        entries = entries * steps_of(own_key, dims, cuts, -0.22, 0.18)
    return jnp.clip(with_spikes(entries, jax.random.fold_in(own_key, 3), *heavy), -most, most).astype(kind)


def setup_inputs(seed: int = 0) -> dict:
    streams_of = jax.random.split(jax.random.key(seed), 6)
    return {
        "ptdf": gaussian_with(streams_of[0], (LINES, BUSES), BUSES ** -0.5, 0.0546875, ((0, 8), (1, 32)), (1, 0, 32, 2.75)),
        "injections": centred(streams_of[1], (BUSES, SCENARIOS), 1.0, 6.0, ((0, 32), (1, 2))),
        "lodf": centred(streams_of[2], (LINES, OUTAGES), 0.5, 3.0, ((0, 256),)),
        "ratings": jnp.clip(jnp.exp(math.log(2.0) - 1.3862944 * jax.random.uniform(streams_of[3], (LINES,), jnp.float32) ** steps_of(streams_of[3], (LINES,), ((0, 256),), -0.2, 0.2)), 0.5, 2.0),
        "outages": draw_outages(jax.random.fold_in(streams_of[5], 71), 0),
    }


softness = 0.2


def overload_sum(base_flow, outage_flow, lodf, ratings):
    lines_here = base_flow.shape[0]
    groups = lines_here // 4

    def line_block(pieces):
        base_rows, lodf_rows, rating_rows = pieces
        post_flow = base_flow_term(base_rows, lodf_rows, outage_flow)
        margin = (jnp.abs(post_flow) - rating_rows[:, None, None]) / (softness * rating_rows[:, None, None])
        return jnp.sum(jax.nn.sigmoid(margin), axis=2)

    summed = lax.map(line_block, (base_flow.reshape(groups, 4, -1), lodf.reshape(groups, 4, -1), ratings.reshape(groups, 4)))
    return summed.reshape(lines_here, -1)


def base_flow_term(base_rows, lodf_rows, outage_flow):
    return base_rows[:, None, :] + lodf_rows.astype(jnp.float32)[:, :, None] * outage_flow[None, :, :]


def reference(ptdf, injections, lodf, ratings, outages):
    base_flow = jnp.dot(ptdf, injections, preferred_element_type=jnp.float32)
    outage_flow = jnp.take(base_flow, outages.astype(jnp.int32), axis=0)
    total = overload_sum(base_flow, outage_flow, lodf, ratings)
    return total / (SCEN_DEV * N_SCEN)
```

```python
import jax
import jax.numpy as jnp
from jax import lax
from jax.experimental import pallas as pl
from jax.experimental.pallas import tpu as pltpu
from jax.sharding import Mesh, PartitionSpec as P

softness = 0.2
PLANE = ("line", "yl")
EXACT = lax.Precision.HIGHEST


def overload_kernel(where_ref, flow_ref, base_ref, lodf_ref, gain_ref, out_ref, spread, rows, turned, scaled):
    lines, scens = base_ref.shape[1], base_ref.shape[0]
    tile = out_ref.shape[1]
    step = pl.program_id(0)

    @pl.when(step == 0)
    def _():
        for line in range(lines):
            spread[line] = jnp.broadcast_to(base_ref[:, line : line + 1], (scens, 128))

    def fetch(group, carry):
        for offset in range(8):
            slot = group * 8 + offset
            rows[pl.ds(slot, 1), :] = flow_ref[pl.ds(where_ref[step * tile + slot], 1), :]
        return carry

    lax.fori_loop(0, tile // 8, fetch, 0)
    for part in range(tile // 128):
        turned[:, part * 128 : part * 128 + 128] = rows[part * 128 : part * 128 + 128, :].T
    scaled[...] = lodf_ref[...].astype(jnp.float32) * gain_ref[...]

    def pair(index, carry):
        first = index * 2
        factors = []
        for j in range(2):
            row = scaled[pl.ds(first + j, 1), :]
            factors.append([jnp.broadcast_to(row[:, k : k + 128], (8, 128)) for k in range(0, tile, 128)])
        sums = [[jnp.zeros((8, 128), jnp.float32) for _ in range(0, tile, 128)] for j in range(2)]
        for s in range(0, scens, 8):
            for part in range(tile // 128):
                flow = turned[s : s + 8, part * 128 : part * 128 + 128]
                for j in range(2):
                    level = spread[first + j, s : s + 8, :] + factors[j][part] * flow
                    sums[j][part] = sums[j][part] + jnp.tanh(jnp.abs(level) - 0.5 / softness)
        for j in range(2):
            out_ref[pl.ds(first + j, 1), :] = jnp.concatenate(
                [jnp.sum(total, axis=0, keepdims=True) for total in sums[j]], axis=1
            )
        return carry

    lax.fori_loop(0, lines // 2, pair, 0)


def overload_sums(where, flow, base, lodf, gain):
    lines, outages = lodf.shape
    scens = base.shape[1]
    tile = min(256, outages)
    return pl.pallas_call(
        overload_kernel,
        out_shape=jax.ShapeDtypeStruct((lines, outages), jnp.float32),
        grid_spec=pltpu.PrefetchScalarGridSpec(
            num_scalar_prefetch=1,
            grid=(outages // tile,),
            in_specs=[
                pl.BlockSpec((outages, scens), lambda i, w: (0, 0), pipeline_mode=pl.Buffered(1)),
                pl.BlockSpec((scens, lines), lambda i, w: (0, 0), pipeline_mode=pl.Buffered(1)),
                pl.BlockSpec((lines, tile), lambda i, w: (0, i)),
                pl.BlockSpec((lines, 1), lambda i, w: (0, 0), pipeline_mode=pl.Buffered(1)),
            ],
            out_specs=pl.BlockSpec((lines, tile), lambda i, w: (0, i)),
            scratch_shapes=[
                pltpu.VMEM((lines, scens, 128), jnp.float32),
                pltpu.VMEM((tile, scens), jnp.float32),
                pltpu.VMEM((scens, tile), jnp.float32),
                pltpu.VMEM((lines, tile), jnp.float32),
            ],
        ),
        compiler_params=pltpu.CompilerParams(vmem_limit_bytes=24 << 20),
        cost_estimate=pl.CostEstimate(
            flops=5 * lines * outages * scens,
            transcendentals=lines * outages * scens,
            bytes_accessed=4 * outages * scens + 6 * lines * outages,
        ),
    )(where, flow, (base * gain).T, lodf, gain)


def exchange(values, axes):
    return lax.all_to_all(values, axes, 0, 0, tiled=True)


def gather_all(rows, axes, members):
    return exchange(jnp.tile(rows, (members, 1)), axes)


def shards(ptdf, injections, lodf, ratings, outages):
    own, count = lodf.shape
    scens = injections.shape[1]
    n_z, n_plane, n_yl = lax.axis_size("z"), lax.axis_size("line") * lax.axis_size("yl"), lax.axis_size("yl")
    column = own * n_z
    share = -(-column // n_plane)
    depth = count // n_plane
    here = lax.axis_index("line") * n_yl + lax.axis_index("yl")

    partial = jnp.dot(ptdf, injections, preferred_element_type=jnp.float32)
    yl = lax.axis_index("yl")
    sent = lax.dynamic_slice_in_dim(partial, (1 - yl) * column, column)
    kept = lax.dynamic_slice_in_dim(partial, yl * column, column)
    flows = kept + lax.ppermute(sent, "yl", [(0, 1), (1, 0)])

    rank = jnp.sum((outages[None, :] < outages[:, None]).astype(jnp.int32), axis=1)
    where = (rank % n_plane) * depth + rank // n_plane
    starts = jnp.sum(
        (outages[None, :] < (column * jnp.arange(n_plane + 1))[:, None]).astype(jnp.int32), axis=1
    )
    lines = here * column + jnp.arange(column)
    before = jnp.sum((outages[None, :] < lines[:, None]).astype(jnp.int32), axis=1)
    through = jnp.sum((outages[None, :] <= lines[:, None]).astype(jnp.int32), axis=1)
    start = jnp.sum((outages < here * column).astype(jnp.int32))
    slot = jnp.where(through > before, (before % n_plane) * share + (before - start) // n_plane, -1)
    deal = (slot[None, :] == jnp.arange(n_plane * share)[:, None]).astype(jnp.float32)

    dealt = exchange(jnp.dot(deal, flows, precision=EXACT), PLANE)
    turn = lax.rem(here - starts[:-1] + count * n_plane, n_plane)[:, None] + n_plane * jnp.arange(share)[None, :]
    place = starts[:-1][:, None] + turn
    place = jnp.where(place < starts[1:][:, None], place // n_plane, -1).reshape(-1)
    collect = (place[None, :] == jnp.arange(depth)[:, None]).astype(jnp.float32)
    collected = jnp.dot(collect, dealt, precision=EXACT)

    both = jnp.concatenate(
        [flows.reshape(n_z, own, scens), collected.reshape(n_z, depth // n_z, scens)], axis=1
    )
    height = own + depth // n_z
    summed = jnp.sum(exchange(both.reshape(n_z * height, scens), "z").reshape(n_z, height, scens), axis=0)
    base = summed[:own]
    class_flow = gather_all(summed[own:], "z", n_z)
    outage_flow = gather_all(class_flow, PLANE, n_plane)

    gain = (0.5 / (softness * ratings))[:, None]
    local = overload_sums(where, outage_flow, base, lodf, gain)
    total = local + lax.ppermute(local, "scen", [(0, 1), (1, 0)])
    return 0.5 + total * (0.5 / (scens * lax.axis_size("scen")))


def solution(mesh):
    n_line, n_bus, n_scen = (mesh.shape[name] for name in ("line", "bus", "scen"))
    split = Mesh(
        mesh.devices.reshape(n_line, 2, n_bus // 2, n_scen), ("line", "yl", "z", "scen")
    )
    return jax.shard_map(
        shards,
        mesh=split,
        in_specs=(
            P("line", ("yl", "z")),
            P(("yl", "z"), "scen"),
            P(("line", "yl", "z"), None),
            P(("line", "yl", "z")),
            P(),
        ),
        out_specs=P(("line", "yl", "z"), None),
        check_vma=False,
    )
```

```python
import jax
import jax.numpy as jnp
from jax import lax
from jax.experimental import pallas as pl
from jax.experimental.pallas import tpu as pltpu
from jax.sharding import Mesh, PartitionSpec as P

softness = 0.2
PLANE = ("line", "yl")
PARTS = 2


def overload_kernel(where_ref, flow_ref, base_ref, lodf_ref, gain_ref, out_ref, spread, rows, turned, scaled):
    lines, scens = base_ref.shape[1], base_ref.shape[0]
    tile = out_ref.shape[1]
    step = pl.program_id(0)
    trips = lines // 2
    per_trip = tile // trips

    def fetch(from_step, first, number):
        for offset in range(number):
            slot = first + offset
            rows[pl.ds(slot, 1), :] = flow_ref[pl.ds(where_ref[from_step * tile + slot], 1), :]

    @pl.when(step == 0)
    def _():
        for line in range(lines):
            spread[line] = jnp.broadcast_to(base_ref[:, line : line + 1], (scens, 128))

        def some(group, carry):
            fetch(0, group * 16, 16)
            return carry

        lax.fori_loop(0, tile // 16, some, 0)

    for part in range(tile // 128):
        turned[:, part * 128 : part * 128 + 128] = rows[part * 128 : part * 128 + 128, :].T
    scaled[...] = lodf_ref[...].astype(jnp.float32) * gain_ref[...]
    ahead = jnp.minimum(step + 1, pl.num_programs(0) - 1)

    def pair(index, carry):
        first = index * 2
        factors = []
        for j in range(2):
            row = scaled[pl.ds(first + j, 1), :]
            factors.append([jnp.broadcast_to(row[:, k : k + 128], (8, 128)) for k in range(0, tile, 128)])
        sums = [[jnp.zeros((8, 128), jnp.float32) for _ in range(0, tile, 128)] for j in range(2)]
        fetch(ahead, index * per_trip, per_trip)
        for s in range(0, scens, 8):
            levels = [spread[first + j, s : s + 8, :] for j in range(2)]
            for part in range(tile // 128):
                flow = turned[s : s + 8, part * 128 : part * 128 + 128]
                for j in range(2):
                    level = levels[j] + factors[j][part] * flow
                    sums[j][part] = sums[j][part] + jnp.tanh(jnp.abs(level) - 0.5 / softness)
        for j in range(2):
            out_ref[pl.ds(first + j, 1), :] = jnp.concatenate(
                [jnp.sum(total, axis=0, keepdims=True) for total in sums[j]], axis=1
            )
        return carry

    lax.fori_loop(0, trips, pair, 0)


def overload_sums(where, flow, base, lodf, gain, part):
    lines = lodf.shape[0]
    outages, scens = flow.shape
    tile = min(256, outages)
    ahead = part * (outages // tile)
    return pl.pallas_call(
        overload_kernel,
        out_shape=jax.ShapeDtypeStruct((lines, outages), jnp.float32),
        grid_spec=pltpu.PrefetchScalarGridSpec(
            num_scalar_prefetch=1,
            grid=(outages // tile,),
            in_specs=[
                pl.BlockSpec((outages, scens), lambda i, w: (0, 0), pipeline_mode=pl.Buffered(1)),
                pl.BlockSpec((scens, lines), lambda i, w: (0, 0), pipeline_mode=pl.Buffered(1)),
                pl.BlockSpec((lines, tile), lambda i, w: (0, i + ahead)),
                pl.BlockSpec((lines, 1), lambda i, w: (0, 0), pipeline_mode=pl.Buffered(1)),
            ],
            out_specs=pl.BlockSpec((lines, tile), lambda i, w: (0, i)),
            scratch_shapes=[
                pltpu.VMEM((lines, scens, 128), jnp.float32),
                pltpu.VMEM((tile, scens), jnp.float32),
                pltpu.VMEM((scens, tile), jnp.float32),
                pltpu.VMEM((lines, tile), jnp.float32),
            ],
        ),
        compiler_params=pltpu.CompilerParams(vmem_limit_bytes=16 << 20),
        cost_estimate=pl.CostEstimate(
            flops=5 * lines * outages * scens,
            transcendentals=lines * outages * scens,
            bytes_accessed=4 * outages * scens + 6 * lines * outages,
        ),
    )(where, flow, base, lodf, gain)


def exchange(values, axes):
    return lax.all_to_all(values, axes, 0, 0, tiled=True)


def gather_all(rows, axes, members):
    return exchange(jnp.tile(rows, (members, 1)), axes)


def select(choice, values):
    high = lax.reduce_precision(values, 8, 7)
    rest = values - high
    middle = lax.reduce_precision(rest, 8, 7)
    pieces = [piece.astype(jnp.bfloat16) for piece in (high, middle, rest - middle)]
    picked = jnp.dot(
        choice.astype(jnp.bfloat16), jnp.concatenate(pieces, axis=1), preferred_element_type=jnp.float32
    )
    width = values.shape[1]
    return picked[:, :width] + (picked[:, width : 2 * width] + picked[:, 2 * width :])


def halve(rows, axis, bit):
    mine = (lax.axis_index(axis) // bit) % 2
    pairs = [(member, member ^ bit) for member in range(lax.axis_size(axis))]
    sent = lax.dynamic_slice_in_dim(rows, 1 - mine, 1, axis=1)
    return lax.dynamic_slice_in_dim(rows, mine, 1, axis=1) + lax.ppermute(sent, axis, pairs)


def below(outages, limits):
    return jnp.sum((outages[None, :] < limits[:, None]).astype(jnp.int32), axis=1)


def shards(ptdf, injections, lodf, ratings, outages):
    own, count = lodf.shape
    scens = injections.shape[1]
    n_line, n_yl, n_z = (lax.axis_size(name) for name in ("line", "yl", "z"))
    n_class = n_line * n_yl
    line, yl = lax.axis_index("line"), lax.axis_index("yl")
    group = ptdf.shape[0]
    column = group // n_yl
    depth = count // PARTS // n_class
    share = -(-(-(-group // n_class) + PARTS) // 8) * 8

    partial = jnp.dot(ptdf, injections, preferred_element_type=jnp.float32)

    pieces = [outages[part * (count // PARTS) : (part + 1) * (count // PARTS)] for part in range(PARTS)]
    edges = group * jnp.arange(n_line + 1)
    lines = line * group + jnp.arange(group)
    slot = jnp.full((group,), -1, jnp.int32)
    used = jnp.zeros((n_line,), jnp.int32)
    here = line * n_yl + yl
    places = jnp.arange(share)[None, :]
    source_row = jnp.full((n_line, share), -1, jnp.int32)
    for part, piece in enumerate(pieces):
        starts = below(piece, edges)
        first, number = starts[:-1], starts[1:] - starts[:-1]
        before, through = below(piece, lines), below(piece, lines + 1)
        mine = before - jnp.sum(jnp.where(jnp.arange(n_line) == line, first, 0))
        offset = jnp.sum(jnp.where(jnp.arange(n_line) == line, used, 0))
        slot = jnp.where(through > before, (before % n_class) * share + offset + mine // n_class, slot)
        turn = places - used[:, None]
        nth = lax.rem(here - first + count * n_class, n_class)[:, None] + n_class * turn
        found = (turn >= 0) & (nth < number[:, None])
        source_row = jnp.where(found, part * depth + (first[:, None] + nth) // n_class, source_row)
        used = used + (number + n_class - 1) // n_class

    deal = slot[None, :] == jnp.arange(n_class * share)[:, None]
    to_classes = select(deal, partial)
    dealt = exchange(to_classes, PLANE)
    to_classes, outages = lax.optimization_barrier((to_classes, outages))
    wheres = []
    for part in range(PARTS):
        piece = outages[part * (count // PARTS) : (part + 1) * (count // PARTS)]
        rank = below(piece, piece)
        wheres.append((rank % n_class) * depth + rank // n_class)
    source_row = jnp.broadcast_to(source_row[:, None, :], (n_line, n_yl, share)).reshape(-1)
    collect = source_row[None, :] == jnp.arange(PARTS * depth)[:, None]
    collected = select(collect, dealt)

    base = halve(partial.reshape(1, n_yl, column, scens), "yl", 1)
    spans = [1 << bit for bit in range(n_z.bit_length() - 1)]

    def halved(base, count):
        for span in [spans.pop(0) for _ in range(min(count, len(spans)))]:
            base = halve(base.reshape(n_z // span // 2, 2, own, scens), "z", span)
        return base

    collected, base = lax.optimization_barrier((collected, halved(base, 1)))
    class_flow = jnp.sum(exchange(collected, "z").reshape(n_z, -1, scens), axis=0)
    class_flow, base = lax.optimization_barrier((class_flow, halved(base, 1)))
    class_flow = gather_all(class_flow, "z", n_z)
    class_flow, base = lax.optimization_barrier((class_flow, halved(base, 1)))
    base = halved(base, len(spans))
    flows = []
    for part in range(PARTS):
        rows = class_flow[part * depth : (part + 1) * depth]
        if part:
            rows, base = lax.optimization_barrier((rows, base))
        flows.append(gather_all(rows, PLANE, n_class))
    base = base.reshape(own, scens)

    gain = (0.5 / (softness * ratings))[:, None]
    scaled_base = (base * gain).T
    totals = []
    for part in range(PARTS):
        local = overload_sums(wheres[part], flows[part], scaled_base, lodf, gain, part)
        totals.append(local + lax.ppermute(local, "scen", [(0, 1), (1, 0)]))
    return 0.5 + jnp.concatenate(totals, axis=1) * (0.5 / (scens * lax.axis_size("scen")))


def solution(mesh):
    n_line, n_bus, n_scen = (mesh.shape[name] for name in ("line", "bus", "scen"))
    split = Mesh(
        mesh.devices.reshape(n_line, 2, n_bus // 2, n_scen), ("line", "yl", "z", "scen")
    )
    return jax.shard_map(
        shards,
        mesh=split,
        in_specs=(
            P("line", ("yl", "z")),
            P(("yl", "z"), "scen"),
            P(("line", "yl", "z"), None),
            P(("line", "yl", "z")),
            P(),
        ),
        out_specs=P(("line", "yl", "z"), None),
        check_vma=False,
    )
```

```python
import jax
import jax.numpy as jnp
from jax import lax
from jax.experimental import pallas as pl
from jax.experimental.pallas import tpu as pltpu
from jax.sharding import Mesh, PartitionSpec as P

softness = 0.2
PLANE = ("line", "yl")
TOGETHER = 4


def overload_kernel(where_ref, flow_ref, base_ref, lodf_ref, gain_ref, out_ref, spread, rows, turned, scaled):
    lines, scens = base_ref.shape
    tile = out_ref.shape[1]
    step = pl.program_id(0)

    @pl.when(step == 0)
    def _():
        columns = (base_ref[...] * gain_ref[...]).T
        for line in range(lines):
            spread[line] = jnp.broadcast_to(columns[:, line : line + 1], (scens, 128))

    def fetch(group, carry):
        for offset in range(32):
            slot = group * 32 + offset
            rows[pl.ds(slot, 1), :] = flow_ref[pl.ds(where_ref[step * tile + slot], 1), :]
        return carry

    lax.fori_loop(0, tile // 32, fetch, 0)
    for part in range(tile // 128):
        turned[:, part * 128 : part * 128 + 128] = rows[part * 128 : part * 128 + 128, :].T
    scaled[...] = lodf_ref[...].astype(jnp.float32) * gain_ref[...]

    def some(index, carry):
        first = index * TOGETHER
        factors = []
        for j in range(TOGETHER):
            row = scaled[pl.ds(first + j, 1), :]
            factors.append([jnp.broadcast_to(row[:, k : k + 128], (8, 128)) for k in range(0, tile, 128)])
        sums = [[jnp.zeros((8, 128), jnp.float32) for _ in range(0, tile, 128)] for j in range(TOGETHER)]
        for s in range(0, scens, 8):
            levels = [spread[first + j, s : s + 8, :] for j in range(TOGETHER)]
            for part in range(tile // 128):
                flow = turned[s : s + 8, part * 128 : part * 128 + 128]
                for j in range(TOGETHER):
                    level = levels[j] + factors[j][part] * flow
                    sums[j][part] = sums[j][part] + jnp.tanh(jnp.abs(level) - 0.5 / softness)
        for j in range(TOGETHER):
            out_ref[pl.ds(first + j, 1), :] = jnp.concatenate(
                [jnp.sum(total, axis=0, keepdims=True) for total in sums[j]], axis=1
            )
        return carry

    lax.fori_loop(0, lines // TOGETHER, some, 0)


def overload_sums(where, flow, base, lodf, gain):
    lines, outages = lodf.shape
    scens = base.shape[1]
    tile = min(256, outages)
    return pl.pallas_call(
        overload_kernel,
        out_shape=jax.ShapeDtypeStruct((lines, outages), jnp.float32),
        grid_spec=pltpu.PrefetchScalarGridSpec(
            num_scalar_prefetch=1,
            grid=(outages // tile,),
            in_specs=[
                pl.BlockSpec((outages, scens), lambda i, w: (0, 0), pipeline_mode=pl.Buffered(1)),
                pl.BlockSpec((lines, scens), lambda i, w: (0, 0), pipeline_mode=pl.Buffered(1)),
                pl.BlockSpec((lines, tile), lambda i, w: (0, i)),
                pl.BlockSpec((lines, 1), lambda i, w: (0, 0), pipeline_mode=pl.Buffered(1)),
            ],
            out_specs=pl.BlockSpec((lines, tile), lambda i, w: (0, i)),
            scratch_shapes=[
                pltpu.VMEM((lines, scens, 128), jnp.float32),
                pltpu.VMEM((tile, scens), jnp.float32),
                pltpu.VMEM((scens, tile), jnp.float32),
                pltpu.VMEM((lines, tile), jnp.float32),
            ],
        ),
        compiler_params=pltpu.CompilerParams(vmem_limit_bytes=16 << 20),
        cost_estimate=pl.CostEstimate(
            flops=5 * lines * outages * scens,
            transcendentals=lines * outages * scens,
            bytes_accessed=4 * outages * scens + 6 * lines * outages,
        ),
    )(where, flow, base, lodf, gain)


def exchange(values, axes):
    return lax.all_to_all(values, axes, 0, 0, tiled=True)


def gather_all(rows, axes, members):
    return exchange(jnp.tile(rows, (members, 1)), axes)


def select(choice, values):
    high = lax.reduce_precision(values, 8, 7)
    rest = values - high
    middle = lax.reduce_precision(rest, 8, 7)
    pieces = [piece.astype(jnp.bfloat16) for piece in (high, middle, rest - middle)]
    picked = jnp.dot(
        choice.astype(jnp.bfloat16), jnp.concatenate(pieces, axis=1), preferred_element_type=jnp.float32
    )
    width = values.shape[1]
    return picked[:, :width] + (picked[:, width : 2 * width] + picked[:, 2 * width :])


def halve(rows, axis, bit):
    mine = (lax.axis_index(axis) // bit) % 2
    pairs = [(member, member ^ bit) for member in range(lax.axis_size(axis))]
    sent = lax.dynamic_slice_in_dim(rows, 1 - mine, 1, axis=1)
    return lax.dynamic_slice_in_dim(rows, mine, 1, axis=1) + lax.ppermute(sent, axis, pairs)


def below(outages, limits):
    return jnp.sum((outages[None, :] < limits[:, None]).astype(jnp.int32), axis=1)


def shards(ptdf, injections, lodf, ratings, outages):
    own, count = lodf.shape
    scens = injections.shape[1]
    n_line, n_yl, n_z = (lax.axis_size(name) for name in ("line", "yl", "z"))
    n_class = n_line * n_yl
    line, yl = lax.axis_index("line"), lax.axis_index("yl")
    here = line * n_yl + yl
    group = ptdf.shape[0]
    column = group // n_yl
    depth = count // n_class
    share = -(-group // n_class)

    starts = below(outages, group * jnp.arange(n_line + 1))
    first, number = starts[:-1], starts[1:] - starts[:-1]
    lines = line * group + jnp.arange(group)
    before, through = below(outages, lines), below(outages, lines + 1)
    mine = before - jnp.sum(jnp.where(jnp.arange(n_line) == line, first, 0))
    slot = jnp.where(through > before, (before % n_class) * share + mine // n_class, -1)
    slot, injections = lax.optimization_barrier((slot, injections))

    partial = jnp.dot(ptdf, injections, preferred_element_type=jnp.float32)
    deal = slot[None, :] == jnp.arange(n_class * share)[:, None]
    to_classes = select(deal, partial)
    dealt = exchange(to_classes, PLANE)
    partial, outages, first, number, to_classes = lax.optimization_barrier(
        (partial, outages, first, number, to_classes)
    )
    nth = lax.rem(here - first + count * n_class, n_class)[:, None] + n_class * jnp.arange(share)[None, :]
    row = jnp.where(nth < number[:, None], (first[:, None] + nth) // n_class, -1)
    row = jnp.broadcast_to(row[:, None, :], (n_line, n_yl, share)).reshape(-1)
    collected = select(row[None, :] == jnp.arange(depth)[:, None], dealt)

    base = halve(partial.reshape(1, n_yl, column, scens), "yl", 1)
    base = halve(base.reshape(n_z // 2, 2, own, scens), "z", 1)
    collected, base = lax.optimization_barrier((collected, base))

    class_flow = jnp.sum(exchange(collected, "z").reshape(n_z, -1, scens), axis=0)
    class_flow = gather_all(class_flow, "z", n_z)
    class_flow, base, outages = lax.optimization_barrier((class_flow, base, outages))
    outage_flow = gather_all(class_flow, PLANE, n_class)
    span = 2
    while span < n_z:
        base = halve(base.reshape(n_z // span // 2, 2, own, scens), "z", span)
        span *= 2
    base = base.reshape(own, scens)
    rank = below(outages, outages)
    where = (rank % n_class) * depth + rank // n_class

    gain = (0.5 / (softness * ratings))[:, None]
    local = overload_sums(where, outage_flow, base, lodf, gain)
    total = local + lax.ppermute(local, "scen", [(0, 1), (1, 0)])
    return 0.5 + total * (0.5 / (scens * lax.axis_size("scen")))


def solution(mesh):
    n_line, n_bus, n_scen = (mesh.shape[name] for name in ("line", "bus", "scen"))
    split = Mesh(
        mesh.devices.reshape(n_line, 2, n_bus // 2, n_scen), ("line", "yl", "z", "scen")
    )
    return jax.shard_map(
        shards,
        mesh=split,
        in_specs=(
            P("line", ("yl", "z")),
            P(("yl", "z"), "scen"),
            P(("line", "yl", "z"), None),
            P(("line", "yl", "z")),
            P(),
        ),
        out_specs=P(("line", "yl", "z"), None),
        check_vma=False,
    )
```

```python
import jax
import jax.numpy as jnp
from jax import lax
from jax.experimental import pallas as pl
from jax.experimental.pallas import tpu as pltpu
from jax.experimental.layout import Layout, with_layout_constraint
from jax.sharding import Mesh, PartitionSpec as P

softness = 0.2
PLANE = ("line", "yl")
TOGETHER = 4


def overload_kernel(where_ref, flow_ref, base_ref, lodf_ref, gain_ref, out_ref, spread, rows, turned, scaled):
    lines, scens = base_ref.shape
    tile = out_ref.shape[1]
    step = pl.program_id(0)

    @pl.when(step == 0)
    def _():
        columns = (base_ref[...] * gain_ref[...]).T
        for line in range(lines):
            spread[line] = jnp.broadcast_to(columns[:, line : line + 1], (scens, 128))

    def fetch(group, carry):
        for offset in range(32):
            slot = group * 32 + offset
            rows[pl.ds(slot, 1), :] = flow_ref[pl.ds(where_ref[step * tile + slot], 1), :]
        return carry

    lax.fori_loop(0, tile // 32, fetch, 0)
    for part in range(tile // 128):
        turned[:, part * 128 : part * 128 + 128] = rows[part * 128 : part * 128 + 128, :].T
    scaled[...] = lodf_ref[...].astype(jnp.float32) * gain_ref[...]

    def some(index, carry):
        first = index * TOGETHER
        factors = []
        for j in range(TOGETHER):
            row = scaled[pl.ds(first + j, 1), :]
            factors.append([jnp.broadcast_to(row[:, k : k + 128], (8, 128)) for k in range(0, tile, 128)])
        sums = [[jnp.zeros((8, 128), jnp.float32) for _ in range(0, tile, 128)] for j in range(TOGETHER)]
        for s in range(0, scens, 8):
            levels = [spread[first + j, s : s + 8, :] for j in range(TOGETHER)]
            for part in range(tile // 128):
                flow = turned[s : s + 8, part * 128 : part * 128 + 128]
                for j in range(TOGETHER):
                    level = levels[j] + factors[j][part] * flow
                    sums[j][part] = sums[j][part] + jnp.tanh(jnp.abs(level) - 0.5 / softness)
        for j in range(TOGETHER):
            out_ref[pl.ds(first + j, 1), :] = jnp.concatenate(
                [jnp.sum(total, axis=0, keepdims=True) for total in sums[j]], axis=1
            )
        return carry

    lax.fori_loop(0, lines // TOGETHER, some, 0)


def overload_sums(where, flow, base, lodf, gain):
    lines, outages = lodf.shape
    scens = base.shape[1]
    tile = min(256, outages)
    return pl.pallas_call(
        overload_kernel,
        out_shape=jax.ShapeDtypeStruct((lines, outages), jnp.float32),
        grid_spec=pltpu.PrefetchScalarGridSpec(
            num_scalar_prefetch=1,
            grid=(outages // tile,),
            in_specs=[
                pl.BlockSpec((outages, scens), lambda i, w: (0, 0), pipeline_mode=pl.Buffered(1)),
                pl.BlockSpec((lines, scens), lambda i, w: (0, 0), pipeline_mode=pl.Buffered(1)),
                pl.BlockSpec((lines, tile), lambda i, w: (0, i)),
                pl.BlockSpec((lines, 1), lambda i, w: (0, 0), pipeline_mode=pl.Buffered(1)),
            ],
            out_specs=pl.BlockSpec((lines, tile), lambda i, w: (0, i)),
            scratch_shapes=[
                pltpu.VMEM((lines, scens, 128), jnp.float32),
                pltpu.VMEM((tile, scens), jnp.float32),
                pltpu.VMEM((scens, tile), jnp.float32),
                pltpu.VMEM((lines, tile), jnp.float32),
            ],
        ),
        compiler_params=pltpu.CompilerParams(vmem_limit_bytes=16 << 20),
        cost_estimate=pl.CostEstimate(
            flops=5 * lines * outages * scens,
            transcendentals=lines * outages * scens,
            bytes_accessed=4 * outages * scens + 6 * lines * outages,
        ),
    )(where, flow, base, lodf, gain)


def exchange(values, axes):
    return lax.all_to_all(values, axes, 0, 0, tiled=True)


def gather_all(rows, axes, members):
    return exchange(jnp.tile(rows, (members, 1)), axes)


def select(choice, values):
    high = lax.reduce_precision(values, 8, 7)
    rest = values - high
    middle = lax.reduce_precision(rest, 8, 7)
    pieces = [piece.astype(jnp.bfloat16) for piece in (high, middle, rest - middle)]
    picked = jnp.dot(
        choice.astype(jnp.bfloat16), jnp.concatenate(pieces, axis=1), preferred_element_type=jnp.float32
    )
    width = values.shape[1]
    return picked[:, :width] + (picked[:, width : 2 * width] + picked[:, 2 * width :])


def carry_over_z(rows, others):
    members, height, scens = rows.shape
    both = jnp.concatenate([rows, others], axis=1)
    both = exchange(both.reshape(-1, scens), "z").reshape(both.shape)
    return both[:, :height], both[:, height:]


def halve(rows, axis, bit):
    mine = (lax.axis_index(axis) // bit) % 2
    pairs = [(member, member ^ bit) for member in range(lax.axis_size(axis))]
    sent = lax.dynamic_slice_in_dim(rows, 1 - mine, 1, axis=1)
    return lax.dynamic_slice_in_dim(rows, mine, 1, axis=1) + lax.ppermute(sent, axis, pairs)


def below(outages, limits):
    return jnp.sum((outages[None, :] < limits[:, None]).astype(jnp.int32), axis=1)


def shards(ptdf, injections, lodf, ratings, outages):
    own, count = lodf.shape
    scens = injections.shape[1]
    n_line, n_yl, n_z = (lax.axis_size(name) for name in ("line", "yl", "z"))
    n_class = n_line * n_yl
    line, yl = lax.axis_index("line"), lax.axis_index("yl")
    here = line * n_yl + yl
    group = ptdf.shape[0]
    column = group // n_yl
    depth = count // n_class
    share = -(-group // n_class)

    starts = below(outages, group * jnp.arange(n_line + 1))
    first, number = starts[:-1], starts[1:] - starts[:-1]
    lines = line * group + jnp.arange(group)
    before, through = below(outages, lines), below(outages, lines + 1)
    mine = before - jnp.sum(jnp.where(jnp.arange(n_line) == line, first, 0))
    slot = jnp.where(through > before, (before % n_class) * share + mine // n_class, -1)
    slot, injections = lax.optimization_barrier((slot, injections))

    partial = jnp.dot(ptdf, injections, preferred_element_type=jnp.float32)
    partial = with_layout_constraint(partial, Layout((0, 1)))
    deal = slot[None, :] == jnp.arange(n_class * share)[:, None]
    to_classes = select(deal, partial)
    dealt = exchange(to_classes, PLANE)
    partial, outages, first, number, to_classes = lax.optimization_barrier(
        (partial, outages, first, number, to_classes)
    )
    nth = lax.rem(here - first + count * n_class, n_class)[:, None] + n_class * jnp.arange(share)[None, :]
    row = jnp.where(nth < number[:, None], (first[:, None] + nth) // n_class, -1)
    row = jnp.broadcast_to(row[:, None, :], (n_line, n_yl, share)).reshape(-1)
    collected = select(row[None, :] == jnp.arange(depth)[:, None], dealt)

    base = halve(partial.reshape(1, n_yl, column, scens), "yl", 1).reshape(n_z, own, scens)
    collected = collected.reshape(n_z, depth // n_z, scens)
    collected, base = lax.optimization_barrier((collected, base))

    class_flow, base_first = carry_over_z(collected, base[:, : own // 2])
    class_flow, base_first = lax.optimization_barrier((jnp.sum(class_flow, axis=0), jnp.sum(base_first, axis=0)))
    class_flow = jnp.broadcast_to(class_flow, collected.shape)
    class_flow, base_second = carry_over_z(class_flow, base[:, own // 2 :])
    class_flow, base_second, outages = lax.optimization_barrier(
        (class_flow.reshape(depth, scens), jnp.sum(base_second, axis=0), outages)
    )
    outage_flow = gather_all(class_flow, PLANE, n_class)
    base = jnp.concatenate([base_first, base_second])
    rank = below(outages, outages)
    where = (rank % n_class) * depth + rank // n_class

    gain = (0.5 / (softness * ratings))[:, None]
    local = overload_sums(where, outage_flow, base, lodf, gain)
    total = local + lax.ppermute(local, "scen", [(0, 1), (1, 0)])
    return 0.5 + total * (0.5 / (scens * lax.axis_size("scen")))


def solution(mesh):
    n_line, n_bus, n_scen = (mesh.shape[name] for name in ("line", "bus", "scen"))
    split = Mesh(
        mesh.devices.reshape(n_line, 2, n_bus // 2, n_scen), ("line", "yl", "z", "scen")
    )
    return jax.shard_map(
        shards,
        mesh=split,
        in_specs=(
            P("line", ("yl", "z")),
            P(("yl", "z"), "scen"),
            P(("line", "yl", "z"), None),
            P(("line", "yl", "z")),
            P(),
        ),
        out_specs=P(("line", "yl", "z"), None),
        check_vma=False,
    )
```

```python
import jax
import jax.numpy as jnp
from jax import lax
from jax.experimental import pallas as pl
from jax.experimental.pallas import tpu as pltpu
from jax.experimental.layout import Layout, with_layout_constraint
from jax.sharding import Mesh, PartitionSpec as P

softness = 0.2
PLANE = ("line", "yl")
TOGETHER = 4


def overload_kernel(where_ref, flow_ref, base_ref, lodf_ref, gain_ref, out_ref, spread, rows, turned, scaled):
    lines, scens = base_ref.shape
    tile = out_ref.shape[1]
    step = pl.program_id(0)

    @pl.when(step == 0)
    def _():
        columns = (base_ref[...] * gain_ref[...]).T
        for line in range(lines):
            spread[line] = jnp.broadcast_to(columns[:, line : line + 1], (scens, 128))

    def fetch(group, carry):
        for offset in range(32):
            slot = group * 32 + offset
            rows[pl.ds(slot, 1), :] = flow_ref[pl.ds(where_ref[step * tile + slot], 1), :]
        return carry

    lax.fori_loop(0, tile // 32, fetch, 0)
    for part in range(tile // 128):
        turned[:, part * 128 : part * 128 + 128] = rows[part * 128 : part * 128 + 128, :].T
    scaled[...] = lodf_ref[...].astype(jnp.float32) * gain_ref[...]

    def some(index, carry):
        first = index * TOGETHER
        factors = []
        for j in range(TOGETHER):
            row = scaled[pl.ds(first + j, 1), :]
            factors.append([jnp.broadcast_to(row[:, k : k + 128], (8, 128)) for k in range(0, tile, 128)])
        sums = [[jnp.zeros((8, 128), jnp.float32) for _ in range(0, tile, 128)] for _ in range(TOGETHER)]
        for s in range(0, scens, 8):
            levels = [spread[first + j, s : s + 8, :] for j in range(TOGETHER)]
            for part in range(tile // 128):
                flow = turned[s : s + 8, part * 128 : part * 128 + 128]
                for j in range(TOGETHER):
                    level = levels[j] + factors[j][part] * flow
                    sums[j][part] = sums[j][part] + jnp.tanh(jnp.abs(level) - 0.5 / softness)
        for j in range(TOGETHER):
            out_ref[pl.ds(first + j, 1), :] = jnp.concatenate(
                [jnp.sum(total, axis=0, keepdims=True) for total in sums[j]], axis=1
            )
        return carry

    lax.fori_loop(0, lines // TOGETHER, some, 0)


def overload_sums(where, flow, base, lodf, gain):
    lines, outages = lodf.shape
    scens = base.shape[1]
    tile = min(256, outages)
    return pl.pallas_call(
        overload_kernel,
        out_shape=jax.ShapeDtypeStruct((lines, outages), jnp.float32),
        grid_spec=pltpu.PrefetchScalarGridSpec(
            num_scalar_prefetch=1,
            grid=(outages // tile,),
            in_specs=[
                pl.BlockSpec((outages, scens), lambda i, w: (0, 0), pipeline_mode=pl.Buffered(1)),
                pl.BlockSpec((lines, scens), lambda i, w: (0, 0), pipeline_mode=pl.Buffered(1)),
                pl.BlockSpec((lines, tile), lambda i, w: (0, i)),
                pl.BlockSpec((lines, 1), lambda i, w: (0, 0), pipeline_mode=pl.Buffered(1)),
            ],
            out_specs=pl.BlockSpec((lines, tile), lambda i, w: (0, i)),
            scratch_shapes=[
                pltpu.VMEM((lines, scens, 128), jnp.float32),
                pltpu.VMEM((tile, scens), jnp.float32),
                pltpu.VMEM((scens, tile), jnp.float32),
                pltpu.VMEM((lines, tile), jnp.float32),
            ],
        ),
        compiler_params=pltpu.CompilerParams(vmem_limit_bytes=16 << 20),
        cost_estimate=pl.CostEstimate(
            flops=5 * lines * outages * scens,
            transcendentals=lines * outages * scens,
            bytes_accessed=4 * outages * scens + 6 * lines * outages,
        ),
    )(where, flow, base, lodf, gain)


def exchange(values, axes):
    return lax.all_to_all(values, axes, 0, 0, tiled=True)


def gather_all(rows, axes, members):
    return exchange(jnp.tile(rows, (members, 1)), axes)


def select(choice, values):
    high = lax.reduce_precision(values, 8, 7)
    rest = values - high
    middle = lax.reduce_precision(rest, 8, 7)
    pieces = [piece.astype(jnp.bfloat16) for piece in (high, middle, rest - middle)]
    picked = jnp.dot(
        choice.astype(jnp.bfloat16), jnp.concatenate(pieces, axis=1), preferred_element_type=jnp.float32
    )
    width = values.shape[1]
    return picked[:, :width] + (picked[:, width : 2 * width] + picked[:, 2 * width :])


def halve(rows, axis, bit):
    mine = (lax.axis_index(axis) // bit) % 2
    pairs = [(member, member ^ bit) for member in range(lax.axis_size(axis))]
    sent = lax.dynamic_slice_in_dim(rows, 1 - mine, 1, axis=1)
    return lax.dynamic_slice_in_dim(rows, mine, 1, axis=1) + lax.ppermute(sent, axis, pairs)


def below(outages, limits):
    return jnp.sum((outages[None, :] < limits[:, None]).astype(jnp.int32), axis=1)


def screen(ptdf, injections, lodf, ratings, outages):
    own, count = lodf.shape
    scens = injections.shape[1]
    n_line, n_yl, n_z = (lax.axis_size(name) for name in ("line", "yl", "z"))
    n_class = n_line * n_yl
    line, yl = lax.axis_index("line"), lax.axis_index("yl")
    here = line * n_yl + yl
    group = ptdf.shape[0]
    column = group // n_yl
    depth = count // n_class
    share = -(-group // n_class)

    starts = below(outages, group * jnp.arange(n_line + 1))
    first, number = starts[:-1], starts[1:] - starts[:-1]
    lines = line * group + jnp.arange(group)
    before, through = below(outages, lines), below(outages, lines + 1)
    mine = before - jnp.sum(jnp.where(jnp.arange(n_line) == line, first, 0))
    slot = jnp.where(through > before, (before % n_class) * share + mine // n_class, -1)
    slot, injections = lax.optimization_barrier((slot, injections))

    partial = jnp.dot(ptdf, injections, preferred_element_type=jnp.float32)
    partial = with_layout_constraint(partial, Layout((0, 1)))
    deal = slot[None, :] == jnp.arange(n_class * share)[:, None]
    to_classes = select(deal, partial)
    dealt = exchange(to_classes, PLANE)
    partial, outages, first, number, to_classes = lax.optimization_barrier(
        (partial, outages, first, number, to_classes)
    )
    nth = lax.rem(here - first + count * n_class, n_class)[:, None] + n_class * jnp.arange(share)[None, :]
    row = jnp.where(nth < number[:, None], (first[:, None] + nth) // n_class, -1)
    row = jnp.broadcast_to(row[:, None, :], (n_line, n_yl, share)).reshape(-1)
    collected = select(row[None, :] == jnp.arange(depth)[:, None], dealt)

    base = halve(partial.reshape(1, n_yl, column, scens), "yl", 1)
    collected, base = lax.optimization_barrier((collected, base))

    base = halve(base.reshape(n_z // 2, 2, own, scens), "z", 1)
    class_flow = exchange(collected, "z")
    class_flow = jnp.sum(class_flow.reshape(n_z, -1, scens), axis=0)
    class_flow, base = lax.optimization_barrier((class_flow, base))
    span = 2
    if span < n_z:
        base = halve(base.reshape(n_z // span // 2, 2, own, scens), "z", span)
        span *= 2
    class_flow = gather_all(class_flow, "z", n_z)
    class_flow, base, outages = lax.optimization_barrier((class_flow, base, outages))
    if span < n_z:
        base = halve(base.reshape(n_z // span // 2, 2, own, scens), "z", span)
        span *= 2
    outage_flow = gather_all(class_flow, PLANE, n_class)
    while span < n_z:
        base = halve(base.reshape(n_z // span // 2, 2, own, scens), "z", span)
        span *= 2
    base = base.reshape(own, scens)
    rank = below(outages, outages)
    where = (rank % n_class) * depth + rank // n_class

    gain = (0.5 / (softness * ratings))[:, None]
    local = overload_sums(where, outage_flow, base, lodf, gain)
    total = local + lax.ppermute(local, "scen", [(0, 1), (1, 0)])
    return 0.5 + total * (0.5 / (scens * lax.axis_size("scen")))


def solution(mesh):
    n_line, n_bus, n_scen = (mesh.shape[name] for name in ("line", "bus", "scen"))
    split = Mesh(
        mesh.devices.reshape(n_line, 2, n_bus // 2, n_scen), ("line", "yl", "z", "scen")
    )
    return jax.shard_map(
        screen,
        mesh=split,
        in_specs=(
            P("line", ("yl", "z")),
            P(("yl", "z"), "scen"),
            P(("line", "yl", "z"), None),
            P(("line", "yl", "z")),
            P(),
        ),
        out_specs=P(("line", "yl", "z"), None),
        check_vma=False,
    )
```
